768 devices in a mesh: wide: 64 (over y, x, core), narrow: 12 (over z).
Axes of the slice: x: 4, y: 8, z: 12, core: 2. Of those that a mesh axis runs over, the one named last changes fastest.
Arguments:
- momentum: bfloat16 [28672, 6144], P('wide', 'narrow'), may hold values from -60 to 60
- gradient: bfloat16 [28672, 6144], P('wide', 'narrow'), may hold values from -6 to 6
- right_prev: float32 [6144, 512], P('narrow'), may hold values from -0.078125 to 0.078125
Outputs:
- momentum_next: bfloat16 [28672, 6144], P('wide', 'narrow')
- weight_update: float32 [28672, 6144], P('wide', 'narrow')
- right_next: float32 [6144, 512], P('narrow')
The draws below stay inside these ranges and needn't reach their ends.
All inputs are finite; a program needn't handle non-finite values.
Results may differ from the reference program's by a relative error of at most 0.009.
Values sent between devices are 32-bit elements; how exact they have to be, the bound alone decides.
A program may use at most 32 MiB of HBM per device.

```python
import math
import jax
import jax.numpy as jnp
from jax import lax

FF = 28672
D = 6144
RANK = 512


def draw_momentum(key, part):
    keys = jax.random.split(jax.random.fold_in(key, 71), 3)
    row_scale = jnp.exp(jax.random.uniform(keys[0], (FF, 1), jnp.float32, -1.15, 1.15))
    col_scale = jnp.exp(jax.random.uniform(keys[1], (1, D), jnp.float32, -1.15, 1.15))
    noise = jnp.clip(jax.random.normal(keys[2], (FF, D), jnp.float32), -5.5, 5.5)
    return (noise * row_scale * col_scale).astype(jnp.bfloat16)


def block_scale(rng, dims, cuts, smallest, top_value):
    def one(axis_at, shards_of):
        heights = jax.random.uniform(jax.random.fold_in(jax.random.fold_in(rng, 6), axis_at), (shards_of,), jnp.float32, smallest / len(cuts), top_value / len(cuts))
        return jnp.repeat(jnp.exp(heights), dims[axis_at] // shards_of).reshape((-1,) + (1,) * (len(dims) - axis_at - 1))

    level = one(*cuts[0])
    for cut in cuts[1:]:
        level = level * one(*cut)
    return level


def bell_draw(own_key, shape, spread, bound, pieces=(), kind=jnp.bfloat16):
    loudness = block_scale(own_key, shape, pieces, -0.22, 0.18) if pieces else 1.0
    values = jax.random.normal(own_key, shape, jnp.float32) * spread * loudness
    return jnp.minimum(jnp.maximum(values, -bound), bound).astype(kind)


def setup_inputs(seed: int = 0) -> dict:
    splits = jax.random.split(jax.random.key(seed), 4)
    return {
        "momentum": draw_momentum(jax.random.fold_in(splits[3], 71), 0),
        "gradient": bell_draw(splits[1], (FF, D), 1.0, 6.0, ((0, 64), (1, 12))),
        "right_prev": bell_draw(splits[2], (D, RANK), D ** -0.5, 0.078125, ((0, 12),), jnp.float32),
    }


def reference(momentum, gradient, right_prev):
    buffer = (momentum.astype(jnp.float32) + gradient.astype(jnp.float32)).astype(jnp.bfloat16)
    projected = jnp.dot(buffer.astype(jnp.float32), right_prev.astype(jnp.bfloat16).astype(jnp.float32), preferred_element_type=jnp.float32)
    gram_matrix = jnp.dot(projected.T, projected, precision=lax.Precision.HIGHEST)
    lower = jnp.linalg.cholesky(gram_matrix)
    left_basis = jax.scipy.linalg.solve_triangular(lower, projected.T, lower=True).T
    right_factor = jnp.dot(buffer.T.astype(jnp.float32), left_basis.astype(jnp.bfloat16).astype(jnp.float32), preferred_element_type=jnp.float32)
    column_squares = lax.optimization_barrier(jnp.sum(right_factor * right_factor, axis=0))
    right_next = right_factor / jnp.sqrt(column_squares + 1e-06)
    feedback = jnp.dot(left_basis, right_factor.T, precision=lax.Precision.HIGHEST)
    momentum_next = (buffer.astype(jnp.float32) - 0.05 * feedback).astype(jnp.bfloat16)
    scaling = math.sqrt(FF * D / RANK)
    weight_update = scaling * jnp.dot(left_basis, right_next.T, precision=lax.Precision.HIGHEST)
    return (momentum_next, weight_update, right_next)
```

```python
import functools
import math

import jax
import jax.numpy as jnp
from jax import lax
from jax.experimental import pallas as pl
from jax.experimental.pallas import tpu as pltpu
from jax.sharding import Mesh
from jax.sharding import PartitionSpec as P

FF = 28672
D = 6144
RANK = 512
BLK = 128
F32 = jnp.float32
BF16 = jnp.bfloat16
NN = ((1,), (0,))
NT = ((1,), (1,))
MESH = pl.DeviceIdType.MESH


def split(x):
    high = x.astype(BF16)
    return high, (x - high.astype(F32)).astype(BF16)


def mm(a, b, dims):
    return lax.dot_general(a, b, (dims, ((), ())), preferred_element_type=F32)


def mm3(a, b, dims):
    (ah, al), (bh, bl) = a, b
    return mm(ah, bh, dims) + (mm(ah, bl, dims) + mm(al, bh, dims))


def lane(x, k):
    return jnp.broadcast_to(x[:, k : k + 1], (8, BLK))


def sublane(x, k):
    return jnp.broadcast_to(x[k : k + 1, :], (8, BLK))


def tree_sum(terms):
    while len(terms) > 1:
        odd = terms[len(terms) & ~1 :]
        terms = [terms[i] + terms[i + 1] for i in range(0, len(terms) & ~1, 2)] + odd
    return terms[0]


def inverse_factor(rows):
    row_id = lax.broadcasted_iota(jnp.int32, (8, BLK), 0)
    lane_id = lax.broadcasted_iota(jnp.int32, (8, BLK), 1)
    count = len(rows)
    a = list(rows)
    e = [(lane_id == row_id + 8 * r).astype(F32) for r in range(count)]
    for r in range(count):
        cols = [lane(a[r], 8 * r + k) for k in range(8)]
        full_a, full_e, forward = a[r], e[r], e[r]
        pivots = jnp.ones((8, BLK), F32)
        for j in range(0, 8, 2):
            p, q, w = sublane(cols[j], j), sublane(cols[j + 1], j), sublane(cols[j + 1], j + 1)
            inv = 1.0 / (p * w - q * q)
            first, second = row_id == j, row_id == j + 1
            pair = first | second
            c1, c2 = cols[j], cols[j + 1]
            m1 = inv * jnp.where(first, -w, jnp.where(second, q, c1 * w - c2 * q))
            m2 = inv * jnp.where(first, q, jnp.where(second, -p, c2 * p - c1 * q))

            def solve(v):
                return jnp.where(pair, 0.0, v) - (m1 * sublane(v, j) + m2 * sublane(v, j + 1))

            ratio = q / p
            f1 = sublane(forward, j)
            f2 = sublane(forward, j + 1)
            below = m1 * f1 + m2 * f2
            forward = forward - jnp.where(
                row_id > j + 1, below, jnp.where(second, ratio * f1, 0.0)
            )
            pivots = jnp.where(first, p, jnp.where(second, w - q * ratio, pivots))
            for k in range(j + 2, 8):
                cols[k] = solve(cols[k])
            full_a, full_e = solve(full_a), solve(full_e)
        e[r] = forward * lax.rsqrt(pivots)
        if r == count - 1:
            break
        row_a = [sublane(full_a, k) for k in range(8)]
        row_e = [sublane(full_e, k) for k in range(8)]
        for s in range(r + 1, count):
            col = [lane(a[s], 8 * r + k) for k in range(8)]
            for k in range(8):
                a[s] = a[s] - col[k] * row_a[k]
                e[s] = e[s] - col[k] * row_e[k]
    return e


class Copies:
    def __init__(self, send, recv):
        self.send, self.recv, self.made = send, recv, {}

    def copy(self, key):
        at, make = self.made[key]
        src, dst, where = make()
        return pltpu.make_async_remote_copy(
            src_ref=src,
            dst_ref=dst,
            send_sem=self.send.at[at],
            recv_sem=self.recv.at[at],
            device_id=where,
            device_id_type=MESH,
        )

    def start(self, key, make):
        self.made[key] = (len(self.made), make)
        self.copy(key).start()

    def arrived(self, key):
        self.copy(key).wait_recv()

    def sent(self):
        for key in self.made:
            self.copy(key).wait_send()


class PlaneSum:
    def __init__(self, sizes, me, part, whole, from_c, from_x, from_y, send, recv):
        self.ny, self.nx, self.nc, _ = sizes
        self.y, self.x, self.c = me
        self.part, self.whole = part, whole
        self.from_c, self.from_x, self.from_y = from_c, from_x, from_y
        rows = part.shape[0]
        self.hc, self.hx, self.hy = rows // 2, rows // 2 // self.nx, rows // 2 // self.nx // self.ny
        self.at_c = self.c * self.hc
        self.at_x = self.at_c + self.x * self.hx
        self.at_y = self.at_x + self.y * self.hy
        self.copies = Copies(send, recv)

    def rows(self, ref, at, count):
        return ref.at[pl.ds(pl.multiple_of(at, 8), count)]

    def send_c(self):
        def make():
            other = (1 - self.c) * self.hc
            return self.rows(self.part, other, self.hc), self.from_c, {"c": 1 - self.c}

        self.copies.start("c", make)

    def deal(self, axis, n, me, at, count, dst):
        for d in range(1, n):

            def make(d=d):
                peer = lax.rem(me + d, n)
                return self.rows(self.part, at + peer * count, count), dst.at[d - 1], {axis: peer}

            self.copies.start((axis, d), make)

    def send_x(self):
        self.copies.arrived("c")
        own = self.rows(self.part, self.at_c, self.hc)
        own[...] += self.from_c[...]
        self.deal("x", self.nx, self.x, self.at_c, self.hx, self.from_x)

    def send_y(self):
        own = self.rows(self.part, self.at_x, self.hx)
        for d in range(1, self.nx):
            self.copies.arrived(("x", d))
        own[...] = tree_sum([own[...]] + [self.from_x[d] for d in range(self.nx - 1)])
        self.deal("y", self.ny, self.y, self.at_x, self.hy, self.from_y)

    def spread(self, axis, n, me, at, count):
        for d in range(1, n):

            def make(d=d):
                block = self.rows(self.whole, at, count)
                return block, block, {axis: lax.rem(me + d, n)}

            self.copies.start((axis + "w", d), make)

    def plane_total(self):
        own = self.rows(self.part, self.at_y, self.hy)
        for d in range(1, self.ny):
            self.copies.arrived(("y", d))
        return tree_sum([own[...]] + [self.from_y[d] for d in range(self.ny - 1)])

    def spread_y(self, total):
        self.whole[pl.ds(pl.multiple_of(self.at_y, 8), self.hy)] = total
        self.spread("y", self.ny, self.y, self.at_y, self.hy)

    def spread_x(self):
        for d in range(1, self.ny):
            self.copies.arrived(("yw", d))
        self.spread("x", self.nx, self.x, self.at_x, self.hx)

    def spread_c(self):
        for d in range(1, self.nx):
            self.copies.arrived(("xw", d))
        self.spread("c", 2, self.c, self.at_c, self.hc)

    def finish(self):
        self.copies.arrived(("cw", 1))
        self.copies.sent()

    @staticmethod
    def count(sizes):
        ny, nx, _, _ = sizes
        return 2 * (1 + (nx - 1) + (ny - 1))


def kernel(
    sizes,
    m_in, g_in, r_in,
    qb_out, fac_out, inv_out,
    m_ref, g_ref, r_ref, buft, part, steps, flat, own, ph, pl_,
    gpart, gwhole, g_c, g_x, g_y, g_own, g_z,
    hpart, hwhole, h_c, h_x, h_y,
    work, inv_blk, qb, fac, squares, others,
    io, zs_send, zs_recv, zg_send, zg_recv, g_send, g_recv, z_send, z_recv,
    h_send, h_recv, q_send, q_recv,
):
    ny, nx, nc, nz = sizes
    y, x, c, z = (lax.axis_index(a) for a in ("y", "x", "c", "z"))
    rows = m_ref.shape[0]
    rank = RANK
    blocks = rank // BLK
    half = rank // 2

    barrier = pltpu.get_barrier_semaphore()
    greeted = 0
    for axis, n, me in (("c", nc, c), ("x", nx, x), ("y", ny, y), ("z", nz, z)):
        for d in range(1, n):
            pl.semaphore_signal(
                barrier, inc=1, device_id={axis: lax.rem(me + d, n)}, device_id_type=MESH
            )
            greeted += 1
    loads = [
        pltpu.make_async_copy(src, dst, io.at[k])
        for k, (src, dst) in enumerate(((m_in, m_ref), (g_in, g_ref), (r_in, r_ref)))
    ]
    for load in loads:
        load.start()
    for load in loads:
        load.wait()

    b = (m_ref[...].astype(F32) + g_ref[...].astype(F32)).astype(BF16)
    chunk = part.shape[0] // nz
    part[0:rows] = mm(b, r_ref[...].astype(BF16), NN)
    if part.shape[0] > rows:
        part[rows:] = jnp.zeros((part.shape[0] - rows, rank), F32)
    pl.semaphore_wait(barrier, greeted)

    tiles = chunk // 8
    cuts = [(int(2 * k >= tiles), 8 * k) for k in range(tiles)]
    longer, shorter = nz // 2, nz - 1 - nz // 2
    hops = lambda way, group: longer if way == group else shorter
    ahead = lambda way, d: lax.rem(z + d, nz) if way == 0 else lax.rem(z + nz - d, nz)
    rows_at = lambda owner, at: pl.ds(pl.multiple_of(owner * chunk + at, 8), 8)
    sums = Copies(zs_send, zs_recv)
    for t in range(1, longer + 1):
        for k, (group, at) in enumerate(cuts):
            for way in range(2):
                length = hops(way, group)
                if t > length:
                    continue
                src = part.at[rows_at(ahead(way, length - t + 1), at)]
                if t > 1:
                    sums.arrived((way, t - 1, k))
                    held = steps.at[way, t - 2, pl.ds(at, 8)]
                    held[...] += src[...]
                    src = held
                dst = steps.at[way, t - 1, pl.ds(at, 8)]
                where = {"z": ahead(way, 1)}
                sums.start((way, t, k), lambda a=src, b=dst, c=where: (a, b, c))
        if t == 1:
            buft[...] = jnp.transpose(b.astype(F32)).astype(BF16)
            work[...] = jnp.zeros((rank, rank), F32)
            own[...] = jnp.zeros((BLK, rank), F32)

    gather = Copies(zg_send, zg_recv)
    for k, (group, at) in enumerate(cuts):
        terms = [part[rows_at(z, at)]]
        for way in range(2):
            length = hops(way, group)
            if length:
                sums.arrived((way, length, k))
                terms.append(steps[way, length - 1, pl.ds(at, 8)])
        total = tree_sum(terms)
        flat[rows_at(z, at)] = total
        own[at : at + 8] = total
        piece = flat.at[rows_at(z, at)]
        for way in range(2):
            if hops(way, group):
                where = {"z": ahead(way, 1)}
                gather.start((way, 1, k), lambda a=piece, c=where: (a, a, c))

    def relay(t):
        for k, (group, at) in enumerate(cuts):
            for way in range(2):
                length = hops(way, group)
                if t > length + 1:
                    continue
                gather.arrived((way, t - 1, k))
                if t <= length:
                    piece = flat.at[rows_at(ahead(1 - way, t - 1), at)]
                    where = {"z": ahead(way, 1)}
                    gather.start((way, t, k), lambda a=piece, c=where: (a, a, c))

    high, low = split(own[...])
    high_t, low_t = split(jnp.transpose(own[...]))
    for top in range(2):
        first = half * top
        gram = mm3(
            (high_t[first : first + half], low_t[first : first + half]),
            (high[:, first:], low[:, first:]),
            NN,
        )
        for k in range((rank - first) // BLK):
            at = top * blocks * half + half * k
            gpart[at : at + half] = gram[:, BLK * k : BLK * (k + 1)]
    gsum = PlaneSum(sizes, (y, x, c), gpart, gwhole, g_c, g_x, g_y, g_send, g_recv)
    hsum = PlaneSum(sizes, (y, x, c), hpart, hwhole, h_c, h_x, h_y, h_send, h_recv)
    gsum.send_c()
    relay(2)
    gsum.send_x()
    for t in range(3, longer + 2):
        if t == 5:
            gsum.send_y()
        if t < longer + 1:
            relay(t)
    if longer + 1 < 6:
        gsum.send_y()
    g_own[...] = gsum.plane_total()
    across = Copies(z_send, z_recv)
    for d in range(1, nz):
        where = {"z": lax.rem(z + d, nz)}
        across.start(d, lambda d=d, c=where: (g_own, g_z.at[d - 1], c))
    if longer > 1:
        relay(longer + 1)

    for k in range(blocks):
        cols = slice(BLK * k, BLK * (k + 1))
        ph[:, cols], pl_[:, cols] = split(flat[0:rows, cols])
    product = mm(buft[...], ph[...], NN) + mm(buft[...], pl_[...], NN)
    for k in range(blocks):
        hpart[rank * k : rank * (k + 1)] = product[:, BLK * k : BLK * (k + 1)]
    hsum.send_c()
    hsum.send_x()
    for d in range(1, nz):
        across.arrived(d)
    gsum.spread_y(tree_sum([g_own[...]] + [g_z[d] for d in range(nz - 1)]))
    hsum.send_y()
    gsum.spread_x()
    hsum.spread_y(hsum.plane_total())
    gsum.spread_c()
    gsum.finish()
    for k in range(blocks):
        work[0:half, BLK * k : BLK * (k + 1)] = gwhole[half * k : half * (k + 1)]
    for k in range(blocks // 2):
        at = blocks * half + half * k
        work[half:rank, half + BLK * k : half + BLK * (k + 1)] = gwhole[at : at + half]

    eye = lax.broadcasted_iota(jnp.int32, (BLK, BLK), 0) == lax.broadcasted_iota(
        jnp.int32, (BLK, BLK), 1
    )

    @pl.loop(0, blocks)
    def _(at):
        r0 = pl.multiple_of(at * BLK, BLK)
        band = pl.ds(r0, BLK)
        diagonal = [work[pl.ds(pl.multiple_of(r0 + 8 * r, 8), 8), band] for r in range(BLK // 8)]
        for r, tile in enumerate(inverse_factor(diagonal)):
            inv_blk[8 * r : 8 * r + 8, :] = tile
        pl.when(at == 0)(hsum.spread_x)
        pl.when(at == 2)(hsum.spread_c)
        work[band, band] = eye.astype(F32)
        solved = mm3(split(inv_blk[...]), split(work[band, :]), NN)
        work[band, :] = solved
        right = split(solved)

        @pl.loop(at + 1, blocks)
        def _(below):
            under = pl.ds(pl.multiple_of(below * BLK, BLK), BLK)
            left = split(jnp.transpose(work[band, under]))
            work[under, band] = jnp.zeros((BLK, BLK), F32)
            work[under, :] -= mm3(left, right, NN)

    block_of = lambda dim: lax.broadcasted_iota(jnp.int32, (rank, rank), dim) // BLK
    inverse = split(jnp.where(block_of(0) >= block_of(1), work[...], 0.0))
    qb[...] = mm3((ph[...], pl_[...]), inverse, NT).astype(BF16)
    stores = [pltpu.make_async_copy(qb, qb_out, io.at[0])]
    stores[0].start()
    hsum.finish()
    whole = jnp.concatenate([hwhole[rank * k : rank * (k + 1)] for k in range(blocks)], axis=1)
    factor = mm3(split(whole), inverse, NT)
    squares[...] = jnp.sum(factor * factor, axis=0, keepdims=True)
    totals = Copies(q_send, q_recv)
    for d in range(1, nz):
        where = {"z": lax.rem(z + d, nz)}
        totals.start(d, lambda d=d, c=where: (squares, others.at[d - 1], c))
    fac[...] = factor
    stores.append(pltpu.make_async_copy(fac, fac_out, io.at[1]))
    stores[1].start()
    for d in range(1, nz):
        totals.arrived(d)
    total = tree_sum([squares[...]] + [others[d] for d in range(nz - 1)])
    inv_out[...] = 1.0 / jnp.sqrt(total + 1e-06)
    for store in stores:
        store.wait()
    for copies in (sums, gather, across, totals):
        copies.sent()


def outputs(m_ref, g_ref, q_ref, f_ref, inv_ref, mn_ref, wu_ref, rn_ref):
    step = pl.program_id(0)
    count = rn_ref.shape[0]
    b = (m_ref[...].astype(F32) + g_ref[...].astype(F32)).astype(BF16)
    feedback = mm(q_ref[...], f_ref[...].astype(BF16), NT)
    mn_ref[...] = (b.astype(F32) - 0.05 * feedback).astype(BF16)
    following = f_ref[...] * inv_ref[...]
    scaling = math.sqrt(FF * D / RANK)
    wu_ref[...] = scaling * mm(q_ref[...], following.astype(BF16), NT)
    rn_ref[...] = f_ref[pl.ds(pl.multiple_of(step * count, 8), count), :] * inv_ref[...]


def body(sizes, momentum, gradient, right_prev):
    ny, nx, nc, nz = sizes
    rows, cols = momentum.shape
    rank = right_prev.shape[1]
    blocks = rank // BLK
    chunk = -(-rows // (8 * nz)) * 8
    longer = nz // 2
    hops = (nz - 1) * (chunk // 8)
    g_rows, h_rows = 3 * rank, blocks * cols
    vmem = pltpu.VMEM

    def plane(count):
        half = count // 2
        return [
            vmem((count, BLK), F32),
            vmem((count, BLK), F32),
            vmem((half, BLK), F32),
            vmem((max(nx - 1, 1), half // nx, BLK), F32),
            vmem((max(ny - 1, 1), half // nx // ny, BLK), F32),
        ]

    def sems(count):
        return [pltpu.SemaphoreType.DMA((count,))] * 2

    piece = g_rows // 2 // nx // ny
    basis, factor, norms = pl.pallas_call(
        functools.partial(kernel, sizes),
        out_shape=(
            jax.ShapeDtypeStruct((rows, rank), BF16),
            jax.ShapeDtypeStruct((cols, rank), F32),
            jax.ShapeDtypeStruct((1, rank), F32),
        ),
        in_specs=[pl.BlockSpec(memory_space=pl.ANY)] * 3,
        out_specs=[pl.BlockSpec(memory_space=pl.ANY)] * 2 + [pl.BlockSpec(memory_space=vmem)],
        scratch_shapes=[
            vmem((rows, cols), BF16),
            vmem((rows, cols), BF16),
            vmem((cols, rank), F32),
            vmem((cols, rows), BF16),
            vmem((chunk * nz, rank), F32),
            vmem((2, longer, chunk, rank), F32),
            vmem((chunk * nz, rank), F32),
            vmem((BLK, rank), F32),
            vmem((rows, rank), BF16),
            vmem((rows, rank), BF16),
            *plane(g_rows),
            vmem((piece, BLK), F32),
            vmem((nz - 1, piece, BLK), F32),
            *plane(h_rows),
            vmem((rank, rank), F32),
            vmem((BLK, BLK), F32),
            vmem((rows, rank), BF16),
            vmem((cols, rank), F32),
            vmem((1, rank), F32),
            vmem((nz - 1, 1, rank), F32),
            pltpu.SemaphoreType.DMA((3,)),
            *sems(hops),
            *sems(hops),
            *sems(PlaneSum.count(sizes)),
            *sems(nz - 1),
            *sems(PlaneSum.count(sizes)),
            *sems(nz - 1),
        ],
        compiler_params=pltpu.CompilerParams(collective_id=0, has_side_effects=True),
    )(momentum, gradient, right_prev)

    parts = 4
    row_block = lambda width: pl.BlockSpec((rows // parts, width), lambda i: (i, 0))
    return pl.pallas_call(
        outputs,
        grid=(parts,),
        out_shape=(
            jax.ShapeDtypeStruct((rows, cols), BF16),
            jax.ShapeDtypeStruct((rows, cols), F32),
            jax.ShapeDtypeStruct((cols, rank), F32),
        ),
        in_specs=[
            row_block(cols),
            row_block(cols),
            row_block(rank),
            pl.BlockSpec((cols, rank), lambda i: (0, 0)),
            pl.BlockSpec((1, rank), lambda i: (0, 0)),
        ],
        out_specs=[
            row_block(cols),
            row_block(cols),
            pl.BlockSpec((cols // parts, rank), lambda i: (i, 0)),
        ],
    )(momentum, gradient, basis, factor, norms)


def solution(mesh):
    sizes = (8, 4, 2, mesh.shape["narrow"])
    torus = Mesh(mesh.devices.reshape(sizes), ("y", "x", "c", "z"))
    wide = ("y", "x", "c")
    in_specs = (P(wide, "z"), P(wide, "z"), P("z", None))
    out_specs = (P(wide, "z"), P(wide, "z"), P("z", None))
    return jax.shard_map(
        functools.partial(body, sizes),
        mesh=torus,
        in_specs=in_specs,
        out_specs=out_specs,
        check_vma=False,
    )
```

```python
import functools
import math

import jax
import jax.numpy as jnp
from jax import lax
from jax.experimental import pallas as pl
from jax.experimental.pallas import tpu as pltpu
from jax.sharding import Mesh
from jax.sharding import PartitionSpec as P

FF = 28672
D = 6144
RANK = 512
BLK = 128
F32 = jnp.float32
BF16 = jnp.bfloat16
NN = ((1,), (0,))
NT = ((1,), (1,))
MESH = pl.DeviceIdType.MESH
PARENT = (None, 0, 1, 2, 2, 4, 4)


def split(x):
    high = x.astype(BF16)
    return high, (x - high.astype(F32)).astype(BF16)


def mm(a, b, dims):
    return lax.dot_general(a, b, (dims, ((), ())), preferred_element_type=F32)


def mm3(a, b, dims):
    (ah, al), (bh, bl) = a, b
    return mm(ah, bh, dims) + (mm(ah, bl, dims) + mm(al, bh, dims))


def lane(x, k):
    return jnp.broadcast_to(x[:, k : k + 1], (8, BLK))


def sublane(x, k):
    return jnp.broadcast_to(x[k : k + 1, :], (8, BLK))


def tree_sum(terms):
    while len(terms) > 1:
        odd = terms[len(terms) & ~1 :]
        terms = [terms[i] + terms[i + 1] for i in range(0, len(terms) & ~1, 2)] + odd
    return terms[0]


def inverse_factor(rows):
    row_id = lax.broadcasted_iota(jnp.int32, (8, BLK), 0)
    lane_id = lax.broadcasted_iota(jnp.int32, (8, BLK), 1)
    count = len(rows)
    a = list(rows)
    e = [(lane_id == row_id + 8 * r).astype(F32) for r in range(count)]
    for r in range(count):
        cols = [lane(a[r], 8 * r + k) for k in range(8)]
        full_a, full_e, forward = a[r], e[r], e[r]
        pivots = jnp.ones((8, BLK), F32)
        for j in range(0, 8, 2):
            p, q, w = sublane(cols[j], j), sublane(cols[j + 1], j), sublane(cols[j + 1], j + 1)
            inv = 1.0 / (p * w - q * q)
            first, second = row_id == j, row_id == j + 1
            pair = first | second
            c1, c2 = cols[j], cols[j + 1]
            m1 = inv * jnp.where(first, -w, jnp.where(second, q, c1 * w - c2 * q))
            m2 = inv * jnp.where(first, q, jnp.where(second, -p, c2 * p - c1 * q))

            def solve(v):
                return jnp.where(pair, 0.0, v) - (m1 * sublane(v, j) + m2 * sublane(v, j + 1))

            ratio = q / p
            f1 = sublane(forward, j)
            f2 = sublane(forward, j + 1)
            below = m1 * f1 + m2 * f2
            forward = forward - jnp.where(
                row_id > j + 1, below, jnp.where(second, ratio * f1, 0.0)
            )
            pivots = jnp.where(first, p, jnp.where(second, w - q * ratio, pivots))
            for k in range(j + 2, 8):
                cols[k] = solve(cols[k])
            full_a, full_e = solve(full_a), solve(full_e)
        e[r] = forward * lax.rsqrt(pivots)
        if r == count - 1:
            break
        row_a = [sublane(full_a, k) for k in range(8)]
        row_e = [sublane(full_e, k) for k in range(8)]
        for s in range(r + 1, count):
            col = [lane(a[s], 8 * r + k) for k in range(8)]
            for k in range(8):
                a[s] = a[s] - col[k] * row_a[k]
                e[s] = e[s] - col[k] * row_e[k]
    return e


class Copies:
    def __init__(self, send, recv):
        self.send, self.recv, self.made = send, recv, {}

    def copy(self, key):
        at, make = self.made[key]
        src, dst, where = make()
        return pltpu.make_async_remote_copy(
            src_ref=src,
            dst_ref=dst,
            send_sem=self.send.at[at],
            recv_sem=self.recv.at[at],
            device_id=where,
            device_id_type=MESH,
        )

    def start(self, key, make):
        self.made[key] = (len(self.made), make)
        self.copy(key).start()

    def arrived(self, key):
        self.copy(key).wait_recv()

    def sent(self):
        for key in self.made:
            self.copy(key).wait_send()


class PlaneSum:
    def __init__(self, sizes, me, part, whole, from_c, from_x, from_y, send, recv):
        self.ny, self.nx, self.nc, _ = sizes
        self.y, self.x, self.c = me
        self.part, self.whole = part, whole
        self.from_c, self.from_x, self.from_y = from_c, from_x, from_y
        rows = part.shape[0]
        self.hc, self.hx, self.hy = rows // 2, rows // 2 // self.nx, rows // 2 // self.nx // self.ny
        self.at_c = self.c * self.hc
        self.at_x = self.at_c + self.x * self.hx
        self.at_y = self.at_x + self.y * self.hy
        self.copies = Copies(send, recv)

    def rows(self, ref, at, count):
        return ref.at[pl.ds(pl.multiple_of(at, 8), count)]

    def send_c(self):
        def make():
            other = (1 - self.c) * self.hc
            return self.rows(self.part, other, self.hc), self.from_c, {"c": 1 - self.c}

        self.copies.start("c", make)

    def deal(self, axis, n, me, at, count, dst):
        for d in range(1, n):

            def make(d=d):
                peer = lax.rem(me + d, n)
                return self.rows(self.part, at + peer * count, count), dst.at[d - 1], {axis: peer}

            self.copies.start((axis, d), make)

    def send_x(self):
        self.copies.arrived("c")
        own = self.rows(self.part, self.at_c, self.hc)
        own[...] += self.from_c[...]
        self.deal("x", self.nx, self.x, self.at_c, self.hx, self.from_x)

    def send_y(self):
        own = self.rows(self.part, self.at_x, self.hx)
        for d in range(1, self.nx):
            self.copies.arrived(("x", d))
        own[...] = tree_sum([own[...]] + [self.from_x[d] for d in range(self.nx - 1)])
        self.deal("y", self.ny, self.y, self.at_x, self.hy, self.from_y)

    def spread(self, axis, n, me, at, count):
        for d in range(1, n):

            def make(d=d):
                block = self.rows(self.whole, at, count)
                return block, block, {axis: lax.rem(me + d, n)}

            self.copies.start((axis + "w", d), make)

    def plane_total(self):
        own = self.rows(self.part, self.at_y, self.hy)
        for d in range(1, self.ny):
            self.copies.arrived(("y", d))
        return tree_sum([own[...]] + [self.from_y[d] for d in range(self.ny - 1)])

    def spread_y(self, total):
        self.whole[pl.ds(pl.multiple_of(self.at_y, 8), self.hy)] = total
        self.spread("y", self.ny, self.y, self.at_y, self.hy)

    def spread_x(self):
        for d in range(1, self.ny):
            self.copies.arrived(("yw", d))
        self.spread("x", self.nx, self.x, self.at_x, self.hx)

    def spread_c(self):
        for d in range(1, self.nx):
            self.copies.arrived(("xw", d))
        self.spread("c", 2, self.c, self.at_c, self.hc)

    def finish(self):
        self.copies.arrived(("cw", 1))
        self.copies.sent()

    @staticmethod
    def count(sizes):
        ny, nx, _, _ = sizes
        return 2 * (1 + (nx - 1) + (ny - 1))


def kernel(
    sizes,
    m_in, g_in, r_in,
    fac_out, fact_out, qb_out, mn_out, inv_out,
    m_ref, g_ref, r_ref, buft, part, steps, flat, own, ph, pl_,
    gpart, gwhole, g_c, g_x, g_y, g_own, g_z,
    hpart, hwhole, h_c, h_x, h_y,
    work, inv_blk, qb, mn, fac, fact, squares, others,
    io, zs_send, zs_recv, zg_send, zg_recv, g_send, g_recv, z_send, z_recv,
    h_send, h_recv, q_send, q_recv,
):
    ny, nx, nc, nz = sizes
    y, x, c, z = (lax.axis_index(a) for a in ("y", "x", "c", "z"))
    rows = m_ref.shape[0]
    rank = RANK
    blocks = rank // BLK
    half = rank // 2

    barrier = pltpu.get_barrier_semaphore()
    greeted = 0
    for axis, n, me in (("c", nc, c), ("x", nx, x), ("y", ny, y), ("z", nz, z)):
        for d in range(1, n):
            pl.semaphore_signal(
                barrier, inc=1, device_id={axis: lax.rem(me + d, n)}, device_id_type=MESH
            )
            greeted += 1
    loads = [
        pltpu.make_async_copy(src, dst, io.at[k])
        for k, (src, dst) in enumerate(((m_in, m_ref), (g_in, g_ref), (r_in, r_ref)))
    ]
    for load in loads:
        load.start()
    for load in loads:
        load.wait()

    b = (m_ref[...].astype(F32) + g_ref[...].astype(F32)).astype(BF16)
    chunk = part.shape[0] // nz
    part[0:rows] = mm(b, r_ref[...].astype(BF16), NN)
    if part.shape[0] > rows:
        part[rows:] = jnp.zeros((part.shape[0] - rows, rank), F32)
    pl.semaphore_wait(barrier, greeted)

    tiles = chunk // 8
    cuts = [(int(2 * k >= tiles), 8 * k) for k in range(tiles)]
    longer, shorter = nz // 2, nz - 1 - nz // 2
    hops = lambda way, group: longer if way == group else shorter
    ahead = lambda way, d: lax.rem(z + d, nz) if way == 0 else lax.rem(z + nz - d, nz)
    rows_at = lambda owner, at: pl.ds(pl.multiple_of(owner * chunk + at, 8), 8)
    sums = Copies(zs_send, zs_recv)
    kids = lambda at, length: [u for u in range(at + 1, length + 1) if PARENT[u] == at]
    for s in (6, 5, 3, 4, 2, 1):
        for k, (group, at) in enumerate(cuts):
            for way in range(2):
                length = hops(way, group)
                if s > length:
                    continue
                src = part.at[rows_at(ahead(way, s), at)]
                below = kids(s, length)
                if below:
                    for u in below:
                        sums.arrived((way, u, k))
                    held = [steps.at[way, u - 1, pl.ds(at, 8)] for u in below]
                    held[0][...] = tree_sum([src[...]] + [h[...] for h in held])
                    src = held[0]
                dst = steps.at[way, s - 1, pl.ds(at, 8)]
                where = {"z": ahead(way, s - PARENT[s])}
                sums.start((way, s, k), lambda a=src, b=dst, c=where: (a, b, c))
        if s == 3:
            buft[...] = jnp.transpose(b.astype(F32)).astype(BF16)
            work[...] = jnp.zeros((rank, rank), F32)
            own[...] = jnp.zeros((BLK, rank), F32)

    gather = Copies(zg_send, zg_recv)

    def relay(s):
        for k, (group, at) in enumerate(cuts):
            for way in range(2):
                length = hops(way, group)
                if s > length:
                    continue
                if s:
                    gather.arrived((way, s, k))
                piece = flat.at[rows_at(ahead(1 - way, s), at)]
                for u in kids(s, length):
                    where = {"z": ahead(way, u - s)}
                    gather.start((way, u, k), lambda a=piece, c=where: (a, a, c))

    for k, (group, at) in enumerate(cuts):
        terms = [part[rows_at(z, at)]]
        for way in range(2):
            if hops(way, group):
                sums.arrived((way, 1, k))
                terms.append(steps[way, 0, pl.ds(at, 8)])
        total = tree_sum(terms)
        flat[rows_at(z, at)] = total
        own[at : at + 8] = total
    relay(0)

    high, low = split(own[...])
    high_t, low_t = split(jnp.transpose(own[...]))
    for top in range(2):
        first = half * top
        gram = mm3(
            (high_t[first : first + half], low_t[first : first + half]),
            (high[:, first:], low[:, first:]),
            NN,
        )
        for k in range((rank - first) // BLK):
            at = top * blocks * half + half * k
            gpart[at : at + half] = gram[:, BLK * k : BLK * (k + 1)]
    gsum = PlaneSum(sizes, (y, x, c), gpart, gwhole, g_c, g_x, g_y, g_send, g_recv)
    hsum = PlaneSum(sizes, (y, x, c), hpart, hwhole, h_c, h_x, h_y, h_send, h_recv)
    gsum.send_c()
    gsum.send_x()
    relay(1)
    gsum.send_y()
    relay(2)
    g_own[...] = gsum.plane_total()
    across = Copies(z_send, z_recv)
    for d in range(1, nz):
        where = {"z": lax.rem(z + d, nz)}
        across.start(d, lambda d=d, c=where: (g_own, g_z.at[d - 1], c))
    for s in (4, 3, 5, 6):
        relay(s)

    for k in range(blocks):
        cols = slice(BLK * k, BLK * (k + 1))
        ph[:, cols], pl_[:, cols] = split(flat[0:rows, cols])
    product = mm(buft[...], ph[...], NN) + mm(buft[...], pl_[...], NN)
    for k in range(blocks):
        hpart[rank * k : rank * (k + 1)] = product[:, BLK * k : BLK * (k + 1)]
    hsum.send_c()
    hsum.send_x()
    for d in range(1, nz):
        across.arrived(d)
    gsum.spread_y(tree_sum([g_own[...]] + [g_z[d] for d in range(nz - 1)]))
    hsum.send_y()
    gsum.spread_x()
    hsum.spread_y(hsum.plane_total())
    gsum.spread_c()
    gsum.finish()
    for k in range(blocks):
        work[0:half, BLK * k : BLK * (k + 1)] = gwhole[half * k : half * (k + 1)]
    for k in range(blocks // 2):
        at = blocks * half + half * k
        work[half:rank, half + BLK * k : half + BLK * (k + 1)] = gwhole[at : at + half]

    eye = lax.broadcasted_iota(jnp.int32, (BLK, BLK), 0) == lax.broadcasted_iota(
        jnp.int32, (BLK, BLK), 1
    )

    @pl.loop(0, blocks)
    def _(at):
        r0 = pl.multiple_of(at * BLK, BLK)
        band = pl.ds(r0, BLK)
        diagonal = [work[pl.ds(pl.multiple_of(r0 + 8 * r, 8), 8), band] for r in range(BLK // 8)]
        for r, tile in enumerate(inverse_factor(diagonal)):
            inv_blk[8 * r : 8 * r + 8, :] = tile
        pl.when(at == 0)(hsum.spread_x)
        pl.when(at == 2)(hsum.spread_c)
        work[band, band] = eye.astype(F32)
        solved = mm3(split(inv_blk[...]), split(work[band, :]), NN)
        work[band, :] = solved
        right = split(solved)

        @pl.loop(at + 1, blocks)
        def _(below):
            under = pl.ds(pl.multiple_of(below * BLK, BLK), BLK)
            left = split(jnp.transpose(work[band, under]))
            work[under, band] = jnp.zeros((BLK, BLK), F32)
            work[under, :] -= mm3(left, right, NN)

    block_of = lambda dim: lax.broadcasted_iota(jnp.int32, (rank, rank), dim) // BLK
    inverse = split(jnp.where(block_of(0) >= block_of(1), work[...], 0.0))
    hsum.finish()
    whole = jnp.concatenate([hwhole[rank * k : rank * (k + 1)] for k in range(blocks)], axis=1)
    factor = mm3(split(whole), inverse, NT)
    squares[...] = jnp.sum(factor * factor, axis=0, keepdims=True)
    totals = Copies(q_send, q_recv)
    for d in range(1, nz):
        where = {"z": lax.rem(z + d, nz)}
        totals.start(d, lambda d=d, c=where: (squares, others.at[d - 1], c))
    fac[...] = factor
    fact[...] = jnp.transpose(factor).astype(BF16)
    qb[...] = mm3((ph[...], pl_[...]), inverse, NT).astype(BF16)
    stores = [
        pltpu.make_async_copy(src, dst, io.at[k])
        for k, (src, dst) in enumerate(
            ((fac, fac_out), (fact, fact_out), (qb, qb_out), (mn, mn_out))
        )
    ]
    for store in stores[:3]:
        store.start()
    b = (m_ref[...].astype(F32) + g_ref[...].astype(F32)).astype(BF16)
    feedback = mm(qb[...], fact[...], NN)
    mn[...] = (b.astype(F32) - 0.05 * feedback).astype(BF16)
    stores[3].start()
    for d in range(1, nz):
        totals.arrived(d)
    total = tree_sum([squares[...]] + [others[d] for d in range(nz - 1)])
    inv_out[...] = 1.0 / jnp.sqrt(total + 1e-06)
    for store in stores:
        store.wait()
    for copies in (sums, gather, across, totals):
        copies.sent()


def outputs(mn_in, q_ref, ft_ref, f_ref, inv_ref, mn_ref, wu_ref, rn_ref):
    inv = inv_ref[...]
    mn_ref[...] = mn_in[...]
    rn_ref[...] = f_ref[...] * inv
    scaled = q_ref[...].astype(F32) * (inv * math.sqrt(FF * D / RANK))
    wu_ref[...] = mm(scaled.astype(BF16), ft_ref[...], NN)


def body(sizes, momentum, gradient, right_prev):
    ny, nx, nc, nz = sizes
    rows, cols = momentum.shape
    rank = right_prev.shape[1]
    blocks = rank // BLK
    chunk = -(-rows // (8 * nz)) * 8
    longer = nz // 2
    hops = (nz - 1) * (chunk // 8)
    g_rows, h_rows = 3 * rank, blocks * cols
    vmem = pltpu.VMEM

    def plane(count):
        half = count // 2
        return [
            vmem((count, BLK), F32),
            vmem((count, BLK), F32),
            vmem((half, BLK), F32),
            vmem((max(nx - 1, 1), half // nx, BLK), F32),
            vmem((max(ny - 1, 1), half // nx // ny, BLK), F32),
        ]

    def sems(count):
        return [pltpu.SemaphoreType.DMA((count,))] * 2

    piece = g_rows // 2 // nx // ny
    factor, factor_t, basis, following, norms = pl.pallas_call(
        functools.partial(kernel, sizes),
        out_shape=(
            jax.ShapeDtypeStruct((cols, rank), F32),
            jax.ShapeDtypeStruct((rank, cols), BF16),
            jax.ShapeDtypeStruct((rows, rank), BF16),
            jax.ShapeDtypeStruct((rows, cols), BF16),
            jax.ShapeDtypeStruct((1, rank), F32),
        ),
        in_specs=[pl.BlockSpec(memory_space=pl.ANY)] * 3,
        out_specs=[pl.BlockSpec(memory_space=pl.ANY)] * 4 + [pl.BlockSpec(memory_space=vmem)],
        scratch_shapes=[
            vmem((rows, cols), BF16),
            vmem((rows, cols), BF16),
            vmem((cols, rank), F32),
            vmem((cols, rows), BF16),
            vmem((chunk * nz, rank), F32),
            vmem((2, longer, chunk, rank), F32),
            vmem((chunk * nz, rank), F32),
            vmem((BLK, rank), F32),
            vmem((rows, rank), BF16),
            vmem((rows, rank), BF16),
            *plane(g_rows),
            vmem((piece, BLK), F32),
            vmem((nz - 1, piece, BLK), F32),
            *plane(h_rows),
            vmem((rank, rank), F32),
            vmem((BLK, BLK), F32),
            vmem((rows, rank), BF16),
            vmem((rows, cols), BF16),
            vmem((cols, rank), F32),
            vmem((rank, cols), BF16),
            vmem((1, rank), F32),
            vmem((nz - 1, 1, rank), F32),
            pltpu.SemaphoreType.DMA((4,)),
            *sems(hops),
            *sems(hops),
            *sems(PlaneSum.count(sizes)),
            *sems(nz - 1),
            *sems(PlaneSum.count(sizes)),
            *sems(nz - 1),
        ],
        compiler_params=pltpu.CompilerParams(collective_id=0, has_side_effects=True),
    )(momentum, gradient, right_prev)

    parts = 4
    row_block = lambda width: pl.BlockSpec((rows // parts, width), lambda i: (i, 0))
    return pl.pallas_call(
        outputs,
        grid=(parts,),
        out_shape=(
            jax.ShapeDtypeStruct((rows, cols), BF16),
            jax.ShapeDtypeStruct((rows, cols), F32),
            jax.ShapeDtypeStruct((cols, rank), F32),
        ),
        in_specs=[
            row_block(cols),
            row_block(rank),
            pl.BlockSpec((rank, cols), lambda i: (0, 0)),
            pl.BlockSpec((cols // parts, rank), lambda i: (i, 0)),
            pl.BlockSpec((1, rank), lambda i: (0, 0)),
        ],
        out_specs=[
            row_block(cols),
            row_block(cols),
            pl.BlockSpec((cols // parts, rank), lambda i: (i, 0)),
        ],
    )(following, basis, factor_t, factor, norms)


def solution(mesh):
    sizes = (8, 4, 2, mesh.shape["narrow"])
    torus = Mesh(mesh.devices.reshape(sizes), ("y", "x", "c", "z"))
    wide = ("y", "x", "c")
    in_specs = (P(wide, "z"), P(wide, "z"), P("z", None))
    out_specs = (P(wide, "z"), P(wide, "z"), P("z", None))
    return jax.shard_map(
        functools.partial(body, sizes),
        mesh=torus,
        in_specs=in_specs,
        out_specs=out_specs,
        check_vma=False,
    )
```

```python
import functools
import math

import jax
import jax.numpy as jnp
from jax import lax
from jax.experimental import pallas as pl
from jax.experimental.pallas import tpu as pltpu
from jax.sharding import Mesh
from jax.sharding import PartitionSpec as P

FF = 28672
D = 6144
RANK = 512
BLK = 128
F32 = jnp.float32
BF16 = jnp.bfloat16
NN = ((1,), (0,))
NT = ((1,), (1,))
MESH = pl.DeviceIdType.MESH
PARENT = (None, 0, 1, 2, 2, 4, 4)


def split(x):
    high = x.astype(BF16)
    return high, (x - high.astype(F32)).astype(BF16)


def mm(a, b, dims):
    return lax.dot_general(a, b, (dims, ((), ())), preferred_element_type=F32)


def mm3(a, b, dims):
    (ah, al), (bh, bl) = a, b
    return mm(ah, bh, dims) + (mm(ah, bl, dims) + mm(al, bh, dims))


def lane(x, k):
    return jnp.broadcast_to(x[:, k : k + 1], (8, BLK))


def sublane(x, k):
    return jnp.broadcast_to(x[k : k + 1, :], (8, BLK))


def tree_sum(terms):
    while len(terms) > 1:
        odd = terms[len(terms) & ~1 :]
        terms = [terms[i] + terms[i + 1] for i in range(0, len(terms) & ~1, 2)] + odd
    return terms[0]


def inverse_factor(rows):
    row_id = lax.broadcasted_iota(jnp.int32, (8, BLK), 0)
    lane_id = lax.broadcasted_iota(jnp.int32, (8, BLK), 1)
    count = len(rows)
    a = list(rows)
    e = [(lane_id == row_id + 8 * r).astype(F32) for r in range(count)]
    for r in range(count):
        cols = [lane(a[r], 8 * r + k) for k in range(8)]
        full_a, full_e, forward = a[r], e[r], e[r]
        pivots = jnp.ones((8, BLK), F32)
        for j in range(0, 8, 2):
            p, q, w = sublane(cols[j], j), sublane(cols[j + 1], j), sublane(cols[j + 1], j + 1)
            inv = 1.0 / (p * w - q * q)
            first, second = row_id == j, row_id == j + 1
            pair = first | second
            c1, c2 = cols[j], cols[j + 1]
            m1 = inv * jnp.where(first, -w, jnp.where(second, q, c1 * w - c2 * q))
            m2 = inv * jnp.where(first, q, jnp.where(second, -p, c2 * p - c1 * q))

            def solve(v):
                return jnp.where(pair, 0.0, v) - (m1 * sublane(v, j) + m2 * sublane(v, j + 1))

            ratio = q / p
            f1 = sublane(forward, j)
            f2 = sublane(forward, j + 1)
            below = m1 * f1 + m2 * f2
            forward = forward - jnp.where(
                row_id > j + 1, below, jnp.where(second, ratio * f1, 0.0)
            )
            pivots = jnp.where(first, p, jnp.where(second, w - q * ratio, pivots))
            for k in range(j + 2, 8):
                cols[k] = solve(cols[k])
            full_a, full_e = solve(full_a), solve(full_e)
        e[r] = forward * lax.rsqrt(pivots)
        if r == count - 1:
            break
        row_a = [sublane(full_a, k) for k in range(8)]
        row_e = [sublane(full_e, k) for k in range(8)]
        for s in range(r + 1, count):
            col = [lane(a[s], 8 * r + k) for k in range(8)]
            for k in range(8):
                a[s] = a[s] - col[k] * row_a[k]
                e[s] = e[s] - col[k] * row_e[k]
    return e


class Copies:
    def __init__(self, send, recv):
        self.send, self.recv, self.made = send, recv, {}

    def copy(self, key):
        at, make = self.made[key]
        src, dst, where = make()
        return pltpu.make_async_remote_copy(
            src_ref=src,
            dst_ref=dst,
            send_sem=self.send.at[at],
            recv_sem=self.recv.at[at],
            device_id=where,
            device_id_type=MESH,
        )

    def start(self, key, make):
        self.made[key] = (len(self.made), make)
        self.copy(key).start()

    def arrived(self, key):
        self.copy(key).wait_recv()

    def sent(self):
        for key in self.made:
            self.copy(key).wait_send()


class PlaneSum:
    def __init__(self, sizes, me, part, whole, from_c, from_x, from_y, send, recv):
        self.ny, self.nx, self.nc, _ = sizes
        self.y, self.x, self.c = me
        self.part, self.whole = part, whole
        self.from_c, self.from_x, self.from_y = from_c, from_x, from_y
        rows = part.shape[0]
        self.hc, self.hx, self.hy = rows // 2, rows // 2 // self.nx, rows // 2 // self.nx // self.ny
        self.at_c = self.c * self.hc
        self.at_x = self.at_c + self.x * self.hx
        self.at_y = self.at_x + self.y * self.hy
        self.copies = Copies(send, recv)

    def rows(self, ref, at, count):
        return ref.at[pl.ds(pl.multiple_of(at, 8), count)]

    def send_c(self):
        def make():
            other = (1 - self.c) * self.hc
            return self.rows(self.part, other, self.hc), self.from_c, {"c": 1 - self.c}

        self.copies.start("c", make)

    def deal(self, axis, n, me, at, count, dst):
        for d in range(1, n):

            def make(d=d):
                peer = lax.rem(me + d, n)
                return self.rows(self.part, at + peer * count, count), dst.at[d - 1], {axis: peer}

            self.copies.start((axis, d), make)

    def send_x(self):
        self.copies.arrived("c")
        own = self.rows(self.part, self.at_c, self.hc)
        own[...] += self.from_c[...]
        self.deal("x", self.nx, self.x, self.at_c, self.hx, self.from_x)

    def send_y(self):
        own = self.rows(self.part, self.at_x, self.hx)
        for d in range(1, self.nx):
            self.copies.arrived(("x", d))
        own[...] = tree_sum([own[...]] + [self.from_x[d] for d in range(self.nx - 1)])
        self.deal("y", self.ny, self.y, self.at_x, self.hy, self.from_y)

    def spread(self, axis, n, me, at, count):
        for d in range(1, n):

            def make(d=d):
                block = self.rows(self.whole, at, count)
                return block, block, {axis: lax.rem(me + d, n)}

            self.copies.start((axis + "w", d), make)

    def plane_total(self):
        own = self.rows(self.part, self.at_y, self.hy)
        for d in range(1, self.ny):
            self.copies.arrived(("y", d))
        return tree_sum([own[...]] + [self.from_y[d] for d in range(self.ny - 1)])

    def spread_y(self, total):
        self.whole[pl.ds(pl.multiple_of(self.at_y, 8), self.hy)] = total
        self.spread("y", self.ny, self.y, self.at_y, self.hy)

    def spread_x(self):
        for d in range(1, self.ny):
            self.copies.arrived(("yw", d))
        self.spread("x", self.nx, self.x, self.at_x, self.hx)

    def spread_c(self):
        for d in range(1, self.nx):
            self.copies.arrived(("xw", d))
        self.spread("c", 2, self.c, self.at_c, self.hc)

    def finish(self):
        self.copies.arrived(("cw", 1))
        self.copies.sent()

    @staticmethod
    def count(sizes):
        ny, nx, _, _ = sizes
        return 2 * (1 + (nx - 1) + (ny - 1))


def kernel(
    sizes,
    m_in, g_in, r_in,
    fac_out, fact_out, qb_out, mn_out, inv_out,
    m_ref, g_ref, r_ref, buft, part, steps, flat, own, ph, pl_,
    ga_part, ga_whole, ga_c, ga_x, ga_y, ga_own, ga_z,
    gb_part, gb_whole, gb_c, gb_x, gb_y, gb_own, gb_z,
    ha_part, ha_whole, ha_c, ha_x, ha_y,
    hb_part, hb_whole, hb_c, hb_x, hb_y,
    work, inv_blk, qb, mn, fac, fact, squares, others,
    io, zs_send, zs_recv, zg_send, zg_recv,
    ga_send, ga_recv, az_send, az_recv, gb_send, gb_recv, bz_send, bz_recv,
    ha_send, ha_recv, hb_send, hb_recv, q_send, q_recv,
):
    ny, nx, nc, nz = sizes
    y, x, c, z = (lax.axis_index(a) for a in ("y", "x", "c", "z"))
    rows = m_ref.shape[0]
    rank = RANK
    blocks = rank // BLK
    half = rank // 2

    barrier = pltpu.get_barrier_semaphore()
    greeted = 0
    for axis, n, me in (("c", nc, c), ("x", nx, x), ("y", ny, y), ("z", nz, z)):
        for d in range(1, n):
            pl.semaphore_signal(
                barrier, inc=1, device_id={axis: lax.rem(me + d, n)}, device_id_type=MESH
            )
            greeted += 1
    loads = [
        pltpu.make_async_copy(src, dst, io.at[k])
        for k, (src, dst) in enumerate(((m_in, m_ref), (g_in, g_ref), (r_in, r_ref)))
    ]
    for load in loads:
        load.start()
    for load in loads:
        load.wait()

    b = (m_ref[...].astype(F32) + g_ref[...].astype(F32)).astype(BF16)
    chunk = part.shape[0] // nz
    part[0:rows] = mm(b, r_ref[...].astype(BF16), NN)
    if part.shape[0] > rows:
        part[rows:] = jnp.zeros((part.shape[0] - rows, rank), F32)
    pl.semaphore_wait(barrier, greeted)

    tiles = chunk // 8
    cuts = [(int(2 * k >= tiles), 8 * k) for k in range(tiles)]
    longer, shorter = nz // 2, nz - 1 - nz // 2
    hops = lambda way, group: longer if way == group else shorter
    ahead = lambda way, d: lax.rem(z + d, nz) if way == 0 else lax.rem(z + nz - d, nz)
    rows_at = lambda owner, at: pl.ds(pl.multiple_of(owner * chunk + at, 8), 8)
    sums = Copies(zs_send, zs_recv)
    kids = lambda at, length: [u for u in range(at + 1, length + 1) if PARENT[u] == at]
    for s in (6, 5, 3, 4, 2, 1):
        for k, (group, at) in enumerate(cuts):
            for way in range(2):
                length = hops(way, group)
                if s > length:
                    continue
                src = part.at[rows_at(ahead(way, s), at)]
                below = kids(s, length)
                if below:
                    for u in below:
                        sums.arrived((way, u, k))
                    held = [steps.at[way, u - 1, pl.ds(at, 8)] for u in below]
                    held[0][...] = tree_sum([src[...]] + [h[...] for h in held])
                    src = held[0]
                dst = steps.at[way, s - 1, pl.ds(at, 8)]
                where = {"z": ahead(way, s - PARENT[s])}
                sums.start((way, s, k), lambda a=src, b=dst, c=where: (a, b, c))
        if s == 3:
            buft[...] = jnp.transpose(b.astype(F32)).astype(BF16)
            work[...] = jnp.zeros((rank, rank), F32)
            own[...] = jnp.zeros((BLK, rank), F32)

    gather = Copies(zg_send, zg_recv)
    for k, (group, at) in enumerate(cuts):
        terms = [part[rows_at(z, at)]]
        for way in range(2):
            if hops(way, group):
                sums.arrived((way, 1, k))
                terms.append(steps[way, 0, pl.ds(at, 8)])
        total = tree_sum(terms)
        flat[rows_at(z, at)] = total
        own[at : at + 8] = total
        piece = flat.at[rows_at(z, at)]
        for way in range(2):
            if hops(way, group):
                where = {"z": ahead(way, 1)}
                gather.start((way, 1, k), lambda a=piece, c=where: (a, a, c))

    def relay(t):
        for k, (group, at) in enumerate(cuts):
            for way in range(2):
                length = hops(way, group)
                if t > length + 1:
                    continue
                gather.arrived((way, t - 1, k))
                if t <= length:
                    piece = flat.at[rows_at(ahead(1 - way, t - 1), at)]
                    where = {"z": ahead(way, 1)}
                    gather.start((way, t, k), lambda a=piece, c=where: (a, a, c))

    high, low = split(own[...])
    high_t, low_t = split(jnp.transpose(own[...]))
    for top, gpart in enumerate((ga_part, gb_part)):
        first = half * top
        gram = mm3(
            (high_t[first : first + half], low_t[first : first + half]),
            (high[:, first:], low[:, first:]),
            NN,
        )
        for k in range((rank - first) // BLK):
            gpart[half * k : half * (k + 1)] = gram[:, BLK * k : BLK * (k + 1)]
    me = (y, x, c)
    ga = PlaneSum(sizes, me, ga_part, ga_whole, ga_c, ga_x, ga_y, ga_send, ga_recv)
    gb = PlaneSum(sizes, me, gb_part, gb_whole, gb_c, gb_x, gb_y, gb_send, gb_recv)
    ha = PlaneSum(sizes, me, ha_part, ha_whole, ha_c, ha_x, ha_y, ha_send, ha_recv)
    hb = PlaneSum(sizes, me, hb_part, hb_whole, hb_c, hb_x, hb_y, hb_send, hb_recv)
    across_a = Copies(az_send, az_recv)
    across_b = Copies(bz_send, bz_recv)

    def send_z(plane, mine, theirs, across):
        mine[...] = plane.plane_total()
        for d in range(1, nz):
            where = {"z": lax.rem(z + d, nz)}
            across.start(d, lambda d=d, c=where: (mine, theirs.at[d - 1], c))

    def total_z(mine, theirs, across):
        for d in range(1, nz):
            across.arrived(d)
        return tree_sum([mine[...]] + [theirs[d] for d in range(nz - 1)])

    ga.send_c()
    gb.send_c()
    relay(2)
    ga.send_x()
    gb.send_x()
    for t in range(3, 4):
        if t < longer + 1:
            relay(t)
    ga.send_y()
    gb.send_y()
    for t in range(4, 6):
        if t < longer + 1:
            relay(t)
    send_z(ga, ga_own, ga_z, across_a)
    for t in range(6, longer + 1):
        relay(t)
    send_z(gb, gb_own, gb_z, across_b)
    relay(longer + 1)

    for k in range(blocks):
        cols = slice(BLK * k, BLK * (k + 1))
        ph[:, cols], pl_[:, cols] = split(flat[0:rows, cols])
    for side, (plane, hpart) in enumerate(((ha, ha_part), (hb, hb_part))):
        cols = slice(half * side, half * (side + 1))
        product = mm(buft[...], ph[:, cols], NN) + mm(buft[...], pl_[:, cols], NN)
        for k in range(blocks // 2):
            hpart[rank * k : rank * (k + 1)] = product[:, BLK * k : BLK * (k + 1)]
        plane.send_c()
    ha.send_x()
    hb.send_x()
    ga.spread_y(total_z(ga_own, ga_z, across_a))
    gb.spread_y(total_z(gb_own, gb_z, across_b))
    ha.send_y()
    ga.spread_x()
    hb.send_y()
    gb.spread_x()
    ga.spread_c()
    ha.spread_y(ha.plane_total())
    hb.spread_y(hb.plane_total())
    ga.finish()
    for k in range(blocks):
        work[0:half, BLK * k : BLK * (k + 1)] = ga_whole[half * k : half * (k + 1)]

    def add_lower():
        gb.finish()
        for k in range(blocks // 2):
            work[half:rank, half + BLK * k : half + BLK * (k + 1)] += gb_whole[
                half * k : half * (k + 1)
            ]

    def spread_x():
        ha.spread_x()
        hb.spread_x()

    def spread_c():
        ha.spread_c()
        hb.spread_c()

    eye = lax.broadcasted_iota(jnp.int32, (BLK, BLK), 0) == lax.broadcasted_iota(
        jnp.int32, (BLK, BLK), 1
    )

    @pl.loop(0, blocks)
    def _(at):
        r0 = pl.multiple_of(at * BLK, BLK)
        band = pl.ds(r0, BLK)
        pl.when(at == 1)(gb.spread_c)
        pl.when(at == blocks // 2)(add_lower)
        diagonal = [work[pl.ds(pl.multiple_of(r0 + 8 * r, 8), 8), band] for r in range(BLK // 8)]
        for r, tile in enumerate(inverse_factor(diagonal)):
            inv_blk[8 * r : 8 * r + 8, :] = tile
        pl.when(at == 1)(spread_x)
        pl.when(at == 3)(spread_c)
        work[band, band] = eye.astype(F32)
        solved = mm3(split(inv_blk[...]), split(work[band, :]), NN)
        work[band, :] = solved
        right = split(solved)

        @pl.loop(at + 1, blocks)
        def _(below):
            under = pl.ds(pl.multiple_of(below * BLK, BLK), BLK)
            left = split(jnp.transpose(work[band, under]))
            work[under, band] = jnp.zeros((BLK, BLK), F32)
            work[under, :] -= mm3(left, right, NN)

    block_of = lambda dim: lax.broadcasted_iota(jnp.int32, (rank, rank), dim) // BLK
    inverse = split(jnp.where(block_of(0) >= block_of(1), work[...], 0.0))
    qb[...] = mm3((ph[...], pl_[...]), inverse, NT).astype(BF16)
    ha.finish()
    hb.finish()
    whole = jnp.concatenate(
        [h[rank * k : rank * (k + 1)] for h in (ha_whole, hb_whole) for k in range(blocks // 2)],
        axis=1,
    )
    factor = mm3(split(whole), inverse, NT)
    squares[...] = jnp.sum(factor * factor, axis=0, keepdims=True)
    totals = Copies(q_send, q_recv)
    for d in range(1, nz):
        where = {"z": lax.rem(z + d, nz)}
        totals.start(d, lambda d=d, c=where: (squares, others.at[d - 1], c))
    fac[...] = factor
    fact[...] = jnp.transpose(factor).astype(BF16)
    stores = [
        pltpu.make_async_copy(src, dst, io.at[k])
        for k, (src, dst) in enumerate(
            ((fac, fac_out), (fact, fact_out), (qb, qb_out), (mn, mn_out))
        )
    ]
    for store in stores[:3]:
        store.start()
    b = (m_ref[...].astype(F32) + g_ref[...].astype(F32)).astype(BF16)
    feedback = mm(qb[...], fact[...], NN)
    mn[...] = (b.astype(F32) - 0.05 * feedback).astype(BF16)
    stores[3].start()
    for d in range(1, nz):
        totals.arrived(d)
    total = tree_sum([squares[...]] + [others[d] for d in range(nz - 1)])
    inv_out[...] = 1.0 / jnp.sqrt(total + 1e-06)
    for store in stores:
        store.wait()
    for copies in (sums, gather, across_a, across_b, totals):
        copies.sent()


def outputs(mn_in, q_ref, ft_ref, f_ref, inv_ref, mn_ref, wu_ref, rn_ref):
    inv = inv_ref[...]
    mn_ref[...] = mn_in[...]
    rn_ref[...] = f_ref[...] * inv
    scaled = q_ref[...].astype(F32) * (inv * math.sqrt(FF * D / RANK))
    wu_ref[...] = mm(scaled.astype(BF16), ft_ref[...], NN)


def body(sizes, momentum, gradient, right_prev):
    ny, nx, nc, nz = sizes
    rows, cols = momentum.shape
    rank = right_prev.shape[1]
    blocks = rank // BLK
    chunk = -(-rows // (8 * nz)) * 8
    longer = nz // 2
    hops = (nz - 1) * (chunk // 8)
    ga_rows, gb_rows, h_rows = 2 * rank, rank, blocks // 2 * cols
    vmem = pltpu.VMEM

    def plane(count):
        half = count // 2
        return [
            vmem((count, BLK), F32),
            vmem((count, BLK), F32),
            vmem((half, BLK), F32),
            vmem((max(nx - 1, 1), half // nx, BLK), F32),
            vmem((max(ny - 1, 1), half // nx // ny, BLK), F32),
        ]

    def sems(count):
        return [pltpu.SemaphoreType.DMA((count,))] * 2

    def crossing(count):
        piece = count // 2 // nx // ny
        return [vmem((piece, BLK), F32), vmem((nz - 1, piece, BLK), F32)]

    factor, factor_t, basis, following, norms = pl.pallas_call(
        functools.partial(kernel, sizes),
        out_shape=(
            jax.ShapeDtypeStruct((cols, rank), F32),
            jax.ShapeDtypeStruct((rank, cols), BF16),
            jax.ShapeDtypeStruct((rows, rank), BF16),
            jax.ShapeDtypeStruct((rows, cols), BF16),
            jax.ShapeDtypeStruct((1, rank), F32),
        ),
        in_specs=[pl.BlockSpec(memory_space=pl.ANY)] * 3,
        out_specs=[pl.BlockSpec(memory_space=pl.ANY)] * 4 + [pl.BlockSpec(memory_space=vmem)],
        scratch_shapes=[
            vmem((rows, cols), BF16),
            vmem((rows, cols), BF16),
            vmem((cols, rank), F32),
            vmem((cols, rows), BF16),
            vmem((chunk * nz, rank), F32),
            vmem((2, longer, chunk, rank), F32),
            vmem((chunk * nz, rank), F32),
            vmem((BLK, rank), F32),
            vmem((rows, rank), BF16),
            vmem((rows, rank), BF16),
            *plane(ga_rows),
            *crossing(ga_rows),
            *plane(gb_rows),
            *crossing(gb_rows),
            *plane(h_rows),
            *plane(h_rows),
            vmem((rank, rank), F32),
            vmem((BLK, BLK), F32),
            vmem((rows, rank), BF16),
            vmem((rows, cols), BF16),
            vmem((cols, rank), F32),
            vmem((rank, cols), BF16),
            vmem((1, rank), F32),
            vmem((nz - 1, 1, rank), F32),
            pltpu.SemaphoreType.DMA((4,)),
            *sems(hops),
            *sems(hops),
            *sems(PlaneSum.count(sizes)),
            *sems(nz - 1),
            *sems(PlaneSum.count(sizes)),
            *sems(nz - 1),
            *sems(PlaneSum.count(sizes)),
            *sems(PlaneSum.count(sizes)),
            *sems(nz - 1),
        ],
        compiler_params=pltpu.CompilerParams(collective_id=0, has_side_effects=True),
    )(momentum, gradient, right_prev)

    parts = 4
    row_block = lambda width: pl.BlockSpec((rows // parts, width), lambda i: (i, 0))
    return pl.pallas_call(
        outputs,
        grid=(parts,),
        out_shape=(
            jax.ShapeDtypeStruct((rows, cols), BF16),
            jax.ShapeDtypeStruct((rows, cols), F32),
            jax.ShapeDtypeStruct((cols, rank), F32),
        ),
        in_specs=[
            row_block(cols),
            row_block(rank),
            pl.BlockSpec((rank, cols), lambda i: (0, 0)),
            pl.BlockSpec((cols // parts, rank), lambda i: (i, 0)),
            pl.BlockSpec((1, rank), lambda i: (0, 0)),
        ],
        out_specs=[
            row_block(cols),
            row_block(cols),
            pl.BlockSpec((cols // parts, rank), lambda i: (i, 0)),
        ],
    )(following, basis, factor_t, factor, norms)


def solution(mesh):
    sizes = (8, 4, 2, mesh.shape["narrow"])
    torus = Mesh(mesh.devices.reshape(sizes), ("y", "x", "c", "z"))
    wide = ("y", "x", "c")
    in_specs = (P(wide, "z"), P(wide, "z"), P("z", None))
    out_specs = (P(wide, "z"), P(wide, "z"), P("z", None))
    return jax.shard_map(
        functools.partial(body, sizes),
        mesh=torus,
        in_specs=in_specs,
        out_specs=out_specs,
        check_vma=False,
    )
```

```python
import functools
import math

import jax
import jax.numpy as jnp
from jax import lax
from jax.experimental import pallas as pl
from jax.experimental.pallas import tpu as pltpu
from jax.sharding import Mesh
from jax.sharding import PartitionSpec as P

FF = 28672
D = 6144
RANK = 512
BLK = 128
F32 = jnp.float32
BF16 = jnp.bfloat16
NN = ((1,), (0,))
NT = ((1,), (1,))
MESH = pl.DeviceIdType.MESH
PARENT = (None, 0, 1, 2, 2, 4, 4)


def split(x):
    high = x.astype(BF16)
    return high, (x - high.astype(F32)).astype(BF16)


def mm(a, b, dims):
    return lax.dot_general(a, b, (dims, ((), ())), preferred_element_type=F32)


def mm3(a, b, dims):
    (ah, al), (bh, bl) = a, b
    return mm(ah, bh, dims) + (mm(ah, bl, dims) + mm(al, bh, dims))


def lane(x, k):
    return jnp.broadcast_to(x[:, k : k + 1], (8, BLK))


def sublane(x, k):
    return jnp.broadcast_to(x[k : k + 1, :], (8, BLK))


def tree_sum(terms):
    while len(terms) > 1:
        odd = terms[len(terms) & ~1 :]
        terms = [terms[i] + terms[i + 1] for i in range(0, len(terms) & ~1, 2)] + odd
    return terms[0]


def inverse_factor(rows):
    row_id = lax.broadcasted_iota(jnp.int32, (8, BLK), 0)
    lane_id = lax.broadcasted_iota(jnp.int32, (8, BLK), 1)
    count = len(rows)
    a = list(rows)
    e = [(lane_id == row_id + 8 * r).astype(F32) for r in range(count)]
    for r in range(count):
        cols = [lane(a[r], 8 * r + k) for k in range(8)]
        full_a, full_e, forward = a[r], e[r], e[r]
        pivots = jnp.ones((8, BLK), F32)
        for j in range(0, 8, 2):
            p, q, w = sublane(cols[j], j), sublane(cols[j + 1], j), sublane(cols[j + 1], j + 1)
            inv = 1.0 / (p * w - q * q)
            first, second = row_id == j, row_id == j + 1
            pair = first | second
            c1, c2 = cols[j], cols[j + 1]
            m1 = inv * jnp.where(first, -w, jnp.where(second, q, c1 * w - c2 * q))
            m2 = inv * jnp.where(first, q, jnp.where(second, -p, c2 * p - c1 * q))

            def solve(v):
                return jnp.where(pair, 0.0, v) - (m1 * sublane(v, j) + m2 * sublane(v, j + 1))

            ratio = q / p
            f1 = sublane(forward, j)
            f2 = sublane(forward, j + 1)
            below = m1 * f1 + m2 * f2
            forward = forward - jnp.where(
                row_id > j + 1, below, jnp.where(second, ratio * f1, 0.0)
            )
            pivots = jnp.where(first, p, jnp.where(second, w - q * ratio, pivots))
            for k in range(j + 2, 8):
                cols[k] = solve(cols[k])
            full_a, full_e = solve(full_a), solve(full_e)
        e[r] = forward * lax.rsqrt(pivots)
        if r == count - 1:
            break
        row_a = [sublane(full_a, k) for k in range(8)]
        row_e = [sublane(full_e, k) for k in range(8)]
        for s in range(r + 1, count):
            col = [lane(a[s], 8 * r + k) for k in range(8)]
            for k in range(8):
                a[s] = a[s] - col[k] * row_a[k]
                e[s] = e[s] - col[k] * row_e[k]
    return e


class Copies:
    def __init__(self, send, recv):
        self.send, self.recv, self.made = send, recv, {}

    def copy(self, key):
        at, make = self.made[key]
        src, dst, where = make()
        return pltpu.make_async_remote_copy(
            src_ref=src,
            dst_ref=dst,
            send_sem=self.send.at[at],
            recv_sem=self.recv.at[at],
            device_id=where,
            device_id_type=MESH,
        )

    def start(self, key, make):
        self.made[key] = (len(self.made), make)
        self.copy(key).start()

    def arrived(self, key):
        self.copy(key).wait_recv()

    def sent(self):
        for key in self.made:
            self.copy(key).wait_send()


class PlaneSum:
    def __init__(self, sizes, me, part, whole, from_c, from_x, from_y, send, recv):
        self.ny, self.nx, self.nc, _ = sizes
        self.y, self.x, self.c = me
        self.part, self.whole = part, whole
        self.from_c, self.from_x, self.from_y = from_c, from_x, from_y
        rows = part.shape[0]
        self.hc, self.hx, self.hy = rows // 2, rows // 2 // self.nx, rows // 2 // self.nx // self.ny
        self.at_c = self.c * self.hc
        self.at_x = self.at_c + self.x * self.hx
        self.at_y = self.at_x + self.y * self.hy
        self.copies = Copies(send, recv)

    def rows(self, ref, at, count):
        return ref.at[pl.ds(pl.multiple_of(at, 8), count)]

    def send_c(self):
        def make():
            other = (1 - self.c) * self.hc
            return self.rows(self.part, other, self.hc), self.from_c, {"c": 1 - self.c}

        self.copies.start("c", make)

    def deal(self, axis, n, me, at, count, dst):
        for d in range(1, n):

            def make(d=d):
                peer = lax.rem(me + d, n)
                return self.rows(self.part, at + peer * count, count), dst.at[d - 1], {axis: peer}

            self.copies.start((axis, d), make)

    def send_x(self):
        self.copies.arrived("c")
        own = self.rows(self.part, self.at_c, self.hc)
        own[...] += self.from_c[...]
        self.deal("x", self.nx, self.x, self.at_c, self.hx, self.from_x)

    def send_y(self):
        own = self.rows(self.part, self.at_x, self.hx)
        for d in range(1, self.nx):
            self.copies.arrived(("x", d))
        own[...] = tree_sum([own[...]] + [self.from_x[d] for d in range(self.nx - 1)])
        self.deal("y", self.ny, self.y, self.at_x, self.hy, self.from_y)

    def spread(self, axis, n, me, at, count):
        for d in range(1, n):

            def make(d=d):
                block = self.rows(self.whole, at, count)
                return block, block, {axis: lax.rem(me + d, n)}

            self.copies.start((axis + "w", d), make)

    def plane_total(self):
        own = self.rows(self.part, self.at_y, self.hy)
        for d in range(1, self.ny):
            self.copies.arrived(("y", d))
        return tree_sum([own[...]] + [self.from_y[d] for d in range(self.ny - 1)])

    def spread_y(self, total):
        self.whole[pl.ds(pl.multiple_of(self.at_y, 8), self.hy)] = total
        self.spread("y", self.ny, self.y, self.at_y, self.hy)

    def spread_x(self):
        for d in range(1, self.ny):
            self.copies.arrived(("yw", d))
        self.spread("x", self.nx, self.x, self.at_x, self.hx)

    def spread_c(self):
        for d in range(1, self.nx):
            self.copies.arrived(("xw", d))
        self.spread("c", 2, self.c, self.at_c, self.hc)

    def finish(self):
        self.copies.arrived(("cw", 1))
        self.copies.sent()

    @staticmethod
    def count(sizes):
        ny, nx, _, _ = sizes
        return 2 * (1 + (nx - 1) + (ny - 1))


def kernel(
    sizes,
    m_in, g_in, r_in,
    fac_out, fact_out, qb_out, mn_out, inv_out,
    m_ref, g_ref, r_ref, buft, part, steps, flat, own, ph, pl_,
    ga_part, ga_whole, ga_c, ga_x, ga_y, ga_own, ga_z,
    gb_part, gb_whole, gb_c, gb_x, gb_y, gb_own, gb_z,
    ha_part, ha_whole, ha_c, ha_x, ha_y,
    hb_part, hb_whole, hb_c, hb_x, hb_y,
    work, inv_blk, qb, mn, fac, fact, squares, others,
    io, zs_send, zs_recv, zg_send, zg_recv,
    ga_send, ga_recv, az_send, az_recv, gb_send, gb_recv, bz_send, bz_recv,
    ha_send, ha_recv, hb_send, hb_recv, q_send, q_recv,
):
    ny, nx, nc, nz = sizes
    y, x, c, z = (lax.axis_index(a) for a in ("y", "x", "c", "z"))
    rows = m_ref.shape[0]
    rank = RANK
    blocks = rank // BLK
    half = rank // 2

    barrier = pltpu.get_barrier_semaphore()
    greeted = 0
    for axis, n, me in (("c", nc, c), ("x", nx, x), ("y", ny, y), ("z", nz, z)):
        for d in range(1, n):
            pl.semaphore_signal(
                barrier, inc=1, device_id={axis: lax.rem(me + d, n)}, device_id_type=MESH
            )
            greeted += 1
    loads = [
        pltpu.make_async_copy(src, dst, io.at[k])
        for k, (src, dst) in enumerate(((m_in, m_ref), (g_in, g_ref), (r_in, r_ref)))
    ]
    for load in loads:
        load.start()
    for load in loads:
        load.wait()

    b = (m_ref[...].astype(F32) + g_ref[...].astype(F32)).astype(BF16)
    chunk = part.shape[0] // nz
    part[0:rows] = mm(b, r_ref[...].astype(BF16), NN)
    if part.shape[0] > rows:
        part[rows:] = jnp.zeros((part.shape[0] - rows, rank), F32)
    pl.semaphore_wait(barrier, greeted)

    tiles = chunk // 8
    cuts = [(int(2 * k >= tiles), 8 * k) for k in range(tiles)]
    longer, shorter = nz // 2, nz - 1 - nz // 2
    hops = lambda way, group: longer if way == group else shorter
    ahead = lambda way, d: lax.rem(z + d, nz) if way == 0 else lax.rem(z + nz - d, nz)
    rows_at = lambda owner, at: pl.ds(pl.multiple_of(owner * chunk + at, 8), 8)
    sums = Copies(zs_send, zs_recv)
    kids = lambda at, length: [u for u in range(at + 1, length + 1) if PARENT[u] == at]
    for s in (6, 5, 3, 4, 2, 1):
        for k, (group, at) in enumerate(cuts):
            for way in range(2):
                length = hops(way, group)
                if s > length:
                    continue
                src = part.at[rows_at(ahead(way, s), at)]
                below = kids(s, length)
                if below:
                    for u in below:
                        sums.arrived((way, u, k))
                    held = [steps.at[way, u - 1, pl.ds(at, 8)] for u in below]
                    held[0][...] = tree_sum([src[...]] + [h[...] for h in held])
                    src = held[0]
                dst = steps.at[way, s - 1, pl.ds(at, 8)]
                where = {"z": ahead(way, s - PARENT[s])}
                sums.start((way, s, k), lambda a=src, b=dst, c=where: (a, b, c))
        if s == 3:
            buft[...] = jnp.transpose(b.astype(F32)).astype(BF16)
            work[...] = jnp.zeros((rank, rank), F32)
            own[...] = jnp.zeros((BLK, rank), F32)

    gather = Copies(zg_send, zg_recv)
    for k, (group, at) in enumerate(cuts):
        terms = [part[rows_at(z, at)]]
        for way in range(2):
            if hops(way, group):
                sums.arrived((way, 1, k))
                terms.append(steps[way, 0, pl.ds(at, 8)])
        total = tree_sum(terms)
        flat[rows_at(z, at)] = total
        own[at : at + 8] = total
        piece = flat.at[rows_at(z, at)]
        for way in range(2):
            if hops(way, group):
                where = {"z": ahead(way, 1)}
                gather.start((way, 1, k), lambda a=piece, c=where: (a, a, c))

    def relay(t):
        for k, (group, at) in enumerate(cuts):
            for way in range(2):
                length = hops(way, group)
                if t > length + 1:
                    continue
                gather.arrived((way, t - 1, k))
                if t <= length:
                    piece = flat.at[rows_at(ahead(1 - way, t - 1), at)]
                    where = {"z": ahead(way, 1)}
                    gather.start((way, t, k), lambda a=piece, c=where: (a, a, c))

    high, low = split(own[...])
    high_t, low_t = split(jnp.transpose(own[...]))
    for top, gpart in enumerate((ga_part, gb_part)):
        first = half * top
        gram = mm3(
            (high_t[first : first + half], low_t[first : first + half]),
            (high[:, first:], low[:, first:]),
            NN,
        )
        for k in range((rank - first) // BLK):
            gpart[half * k : half * (k + 1)] = gram[:, BLK * k : BLK * (k + 1)]
    me = (y, x, c)
    ga = PlaneSum(sizes, me, ga_part, ga_whole, ga_c, ga_x, ga_y, ga_send, ga_recv)
    gb = PlaneSum(sizes, me, gb_part, gb_whole, gb_c, gb_x, gb_y, gb_send, gb_recv)
    ha = PlaneSum(sizes, me, ha_part, ha_whole, ha_c, ha_x, ha_y, ha_send, ha_recv)
    hb = PlaneSum(sizes, me, hb_part, hb_whole, hb_c, hb_x, hb_y, hb_send, hb_recv)
    across_a = Copies(az_send, az_recv)
    across_b = Copies(bz_send, bz_recv)

    def send_z(plane, mine, theirs, across):
        mine[...] = plane.plane_total()
        for d in range(1, nz):
            where = {"z": lax.rem(z + d, nz)}
            across.start(d, lambda d=d, c=where: (mine, theirs.at[d - 1], c))

    def total_z(mine, theirs, across):
        for d in range(1, nz):
            across.arrived(d)
        return tree_sum([mine[...]] + [theirs[d] for d in range(nz - 1)])

    ga.send_c()
    gb.send_c()
    relay(2)
    ga.send_x()
    gb.send_x()
    for t in range(3, 4):
        if t < longer + 1:
            relay(t)
    ga.send_y()
    gb.send_y()
    for t in range(4, 6):
        if t < longer + 1:
            relay(t)
    send_z(ga, ga_own, ga_z, across_a)
    for t in range(6, longer + 1):
        relay(t)
    send_z(gb, gb_own, gb_z, across_b)
    relay(longer + 1)

    for k in range(blocks):
        cols = slice(BLK * k, BLK * (k + 1))
        ph[:, cols], pl_[:, cols] = split(flat[0:rows, cols])
    for side, (plane, hpart) in enumerate(((ha, ha_part), (hb, hb_part))):
        cols = slice(half * side, half * (side + 1))
        product = mm(buft[...], ph[:, cols], NN) + mm(buft[...], pl_[:, cols], NN)
        for k in range(blocks // 2):
            hpart[rank * k : rank * (k + 1)] = product[:, BLK * k : BLK * (k + 1)]
        plane.send_c()
    ga.spread_y(total_z(ga_own, ga_z, across_a))
    ha.send_x()
    gb.spread_y(total_z(gb_own, gb_z, across_b))
    hb.send_x()
    ga.spread_x()
    ha.send_y()
    hb.send_y()
    gb.spread_x()
    ga.spread_c()
    ha.spread_y(ha.plane_total())
    hb.spread_y(hb.plane_total())
    ga.finish()
    for k in range(blocks):
        work[0:half, BLK * k : BLK * (k + 1)] = ga_whole[half * k : half * (k + 1)]

    def add_lower():
        gb.finish()
        for k in range(blocks // 2):
            work[half:rank, half + BLK * k : half + BLK * (k + 1)] += gb_whole[
                half * k : half * (k + 1)
            ]

    def spread_x():
        ha.spread_x()
        hb.spread_x()

    def spread_c():
        ha.spread_c()
        hb.spread_c()

    eye = lax.broadcasted_iota(jnp.int32, (BLK, BLK), 0) == lax.broadcasted_iota(
        jnp.int32, (BLK, BLK), 1
    )

    @pl.loop(0, blocks)
    def _(at):
        r0 = pl.multiple_of(at * BLK, BLK)
        band = pl.ds(r0, BLK)
        pl.when(at == 1)(gb.spread_c)
        pl.when(at == blocks // 2)(add_lower)
        diagonal = [work[pl.ds(pl.multiple_of(r0 + 8 * r, 8), 8), band] for r in range(BLK // 8)]
        for r, tile in enumerate(inverse_factor(diagonal)):
            inv_blk[8 * r : 8 * r + 8, :] = tile
        pl.when(at == 1)(spread_x)
        pl.when(at == 3)(spread_c)
        work[band, band] = eye.astype(F32)
        solved = mm3(split(inv_blk[...]), split(work[band, :]), NN)
        work[band, :] = solved
        right = split(solved)

        @pl.loop(at + 1, blocks)
        def _(below):
            under = pl.ds(pl.multiple_of(below * BLK, BLK), BLK)
            left = split(jnp.transpose(work[band, under]))
            work[under, band] = jnp.zeros((BLK, BLK), F32)
            work[under, :] -= mm3(left, right, NN)

    block_of = lambda dim: lax.broadcasted_iota(jnp.int32, (rank, rank), dim) // BLK
    inverse = split(jnp.where(block_of(0) >= block_of(1), work[...], 0.0))
    qb[...] = mm3((ph[...], pl_[...]), inverse, NT).astype(BF16)
    ha.finish()
    hb.finish()
    whole = jnp.concatenate(
        [h[rank * k : rank * (k + 1)] for h in (ha_whole, hb_whole) for k in range(blocks // 2)],
        axis=1,
    )
    factor = mm3(split(whole), inverse, NT)
    squares[...] = jnp.sum(factor * factor, axis=0, keepdims=True)
    totals = Copies(q_send, q_recv)
    for d in range(1, nz):
        where = {"z": lax.rem(z + d, nz)}
        totals.start(d, lambda d=d, c=where: (squares, others.at[d - 1], c))
    fac[...] = factor
    fact[...] = jnp.transpose(factor).astype(BF16)
    stores = [
        pltpu.make_async_copy(src, dst, io.at[k])
        for k, (src, dst) in enumerate(
            ((fac, fac_out), (fact, fact_out), (qb, qb_out), (mn, mn_out))
        )
    ]
    for store in stores[:3]:
        store.start()
    b = (m_ref[...].astype(F32) + g_ref[...].astype(F32)).astype(BF16)
    feedback = mm(qb[...], fact[...], NN)
    mn[...] = (b.astype(F32) - 0.05 * feedback).astype(BF16)
    stores[3].start()
    for d in range(1, nz):
        totals.arrived(d)
    total = tree_sum([squares[...]] + [others[d] for d in range(nz - 1)])
    inv_out[...] = 1.0 / jnp.sqrt(total + 1e-06)
    for store in stores:
        store.wait()
    for copies in (sums, gather, across_a, across_b, totals):
        copies.sent()


def outputs(mn_in, q_ref, ft_ref, f_ref, inv_ref, mn_ref, wu_ref, rn_ref):
    inv = inv_ref[...]
    mn_ref[...] = mn_in[...]
    rn_ref[...] = f_ref[...] * inv
    scaled = q_ref[...].astype(F32) * (inv * math.sqrt(FF * D / RANK))
    wu_ref[...] = mm(scaled.astype(BF16), ft_ref[...], NN)


def body(sizes, momentum, gradient, right_prev):
    ny, nx, nc, nz = sizes
    rows, cols = momentum.shape
    rank = right_prev.shape[1]
    blocks = rank // BLK
    chunk = -(-rows // (8 * nz)) * 8
    longer = nz // 2
    hops = (nz - 1) * (chunk // 8)
    ga_rows, gb_rows, h_rows = 2 * rank, rank, blocks // 2 * cols
    vmem = pltpu.VMEM

    def plane(count):
        half = count // 2
        return [
            vmem((count, BLK), F32),
            vmem((count, BLK), F32),
            vmem((half, BLK), F32),
            vmem((max(nx - 1, 1), half // nx, BLK), F32),
            vmem((max(ny - 1, 1), half // nx // ny, BLK), F32),
        ]

    def sems(count):
        return [pltpu.SemaphoreType.DMA((count,))] * 2

    def crossing(count):
        piece = count // 2 // nx // ny
        return [vmem((piece, BLK), F32), vmem((nz - 1, piece, BLK), F32)]

    factor, factor_t, basis, following, norms = pl.pallas_call(
        functools.partial(kernel, sizes),
        out_shape=(
            jax.ShapeDtypeStruct((cols, rank), F32),
            jax.ShapeDtypeStruct((rank, cols), BF16),
            jax.ShapeDtypeStruct((rows, rank), BF16),
            jax.ShapeDtypeStruct((rows, cols), BF16),
            jax.ShapeDtypeStruct((1, rank), F32),
        ),
        in_specs=[pl.BlockSpec(memory_space=pl.ANY)] * 3,
        out_specs=[pl.BlockSpec(memory_space=pl.ANY)] * 4 + [pl.BlockSpec(memory_space=vmem)],
        scratch_shapes=[
            vmem((rows, cols), BF16),
            vmem((rows, cols), BF16),
            vmem((cols, rank), F32),
            vmem((cols, rows), BF16),
            vmem((chunk * nz, rank), F32),
            vmem((2, longer, chunk, rank), F32),
            vmem((chunk * nz, rank), F32),
            vmem((BLK, rank), F32),
            vmem((rows, rank), BF16),
            vmem((rows, rank), BF16),
            *plane(ga_rows),
            *crossing(ga_rows),
            *plane(gb_rows),
            *crossing(gb_rows),
            *plane(h_rows),
            *plane(h_rows),
            vmem((rank, rank), F32),
            vmem((BLK, BLK), F32),
            vmem((rows, rank), BF16),
            vmem((rows, cols), BF16),
            vmem((cols, rank), F32),
            vmem((rank, cols), BF16),
            vmem((1, rank), F32),
            vmem((nz - 1, 1, rank), F32),
            pltpu.SemaphoreType.DMA((4,)),
            *sems(hops),
            *sems(hops),
            *sems(PlaneSum.count(sizes)),
            *sems(nz - 1),
            *sems(PlaneSum.count(sizes)),
            *sems(nz - 1),
            *sems(PlaneSum.count(sizes)),
            *sems(PlaneSum.count(sizes)),
            *sems(nz - 1),
        ],
        compiler_params=pltpu.CompilerParams(collective_id=0, has_side_effects=True),
    )(momentum, gradient, right_prev)

    parts = 4
    row_block = lambda width: pl.BlockSpec((rows // parts, width), lambda i: (i, 0))
    return pl.pallas_call(
        outputs,
        grid=(parts,),
        out_shape=(
            jax.ShapeDtypeStruct((rows, cols), BF16),
            jax.ShapeDtypeStruct((rows, cols), F32),
            jax.ShapeDtypeStruct((cols, rank), F32),
        ),
        in_specs=[
            row_block(cols),
            row_block(rank),
            pl.BlockSpec((rank, cols), lambda i: (0, 0)),
            pl.BlockSpec((cols // parts, rank), lambda i: (i, 0)),
            pl.BlockSpec((1, rank), lambda i: (0, 0)),
        ],
        out_specs=[
            row_block(cols),
            row_block(cols),
            pl.BlockSpec((cols // parts, rank), lambda i: (i, 0)),
        ],
    )(following, basis, factor_t, factor, norms)


def solution(mesh):
    sizes = (8, 4, 2, mesh.shape["narrow"])
    torus = Mesh(mesh.devices.reshape(sizes), ("y", "x", "c", "z"))
    wide = ("y", "x", "c")
    in_specs = (P(wide, "z"), P(wide, "z"), P("z", None))
    out_specs = (P(wide, "z"), P(wide, "z"), P("z", None))
    return jax.shard_map(
        functools.partial(body, sizes),
        mesh=torus,
        in_specs=in_specs,
        out_specs=out_specs,
        check_vma=False,
    )
```
